32 devices in a mesh: lat: 4 (over y, x), lon: 8 (over z, core).
Axes of the slice: x: 2, y: 2, z: 4, core: 2. Of those that a mesh axis runs over, the one named last changes fastest.
Arguments:
- forcing: float32 [2, 2, 8, 64, 64], P(None, None, None, 'lat', 'lon'), may hold values from -6 to 6
- zonal: float32 [8, 64, 64], P(None, 'lat', 'lon'), may hold values from -0.3 to 0.3
- meridional: float32 [8, 64, 64], P(None, 'lat', 'lon'), may hold values from -0.3 to 0.3
- mixing: float32 [7, 64, 64], P(None, 'lat', 'lon'), may hold values from 0.03 to 0.24
- panel: bfloat16 [4096, 4, 1024], P('lat', None, 'lon'), may hold values from -0.125 to 0.125
Outputs:
- adjoint_state: float32 [2, 8, 64, 64], P(None, None, 'lat', 'lon')
- state_grad: float32 [2, 8, 4, 1024], P(None, None, 'lat', 'lon')
- flux_grad: float32 [2, 4, 1024], P(None, 'lat', 'lon')
The draws below stay inside these ranges and needn't reach their ends.
All inputs are finite; a program needn't handle non-finite values.
Results may differ from the reference program's by a relative error of at most 0.0029.
Values may be sent and summed in bfloat16 or wider, within the bound.
No kernel may reach another device: no remote copies, remote signals or barrier semaphores. Data moves between devices by JAX's collectives and lax.ppermute only.
A program may use at most 64 MiB of HBM per device.

```python
import math
import jax
import jax.numpy as jnp
from jax import lax

CLAT = 16
CLON = 8
LEV = 8
NLAT = 64
NLON = 64
ORDER = 4096
GCOLS = 1024
N_LAT = 4


def spiked(values, rng, source, target, blocks, factor):
    owner, partner = [(jnp.arange(values.shape[axis_at]) // (values.shape[axis_at] // blocks)).reshape([-1 if axis == axis_at else 1 for axis in range(values.ndim)]) for axis_at in (source, target)]
    chosen = jax.random.permutation(rng, blocks)[partner]
    strong = (owner == chosen) | (owner == (partner + blocks // 2) % blocks)
    return jnp.where(strong, factor * values, values)


def shard_levels(stream_key, dims, cuts, least, largest):
    level, own = 1.0, jax.random.fold_in(stream_key, 6)
    for axis_at, blocks in cuts:
        steps = jnp.exp(jax.random.uniform(jax.random.fold_in(own, axis_at), (blocks,), jnp.float32, least / len(cuts), largest / len(cuts)))
        level = level * jnp.repeat(steps, dims[axis_at] // blocks).reshape([-1 if axis == axis_at else 1 for axis in range(len(dims))])
    return level


def gaussian(key, dims, spread, limit, pieces=(), kind=jnp.bfloat16):
    drawn = jax.random.normal(key, dims, jnp.float32) * spread
    if len(pieces) > 0:
        drawn = shard_levels(key, dims, pieces, -0.22, 0.18) * drawn
    return jnp.clip(drawn, min=-limit, max=limit).astype(kind)


def noise_with(stream_key, extent, width, limit, pieces, heavy, held_as=jnp.bfloat16):
    drawn = width * jax.random.normal(stream_key, extent, jnp.float32)
    if pieces:
        drawn = drawn * shard_levels(stream_key, extent, pieces, -0.22, 0.18)
    return jnp.clip(spiked(drawn, jax.random.fold_in(stream_key, 3), *heavy), -limit, limit).astype(held_as)


def setup_inputs(seed: int = 0) -> dict:
    arg_keys = jax.random.split(jax.random.key(seed), 6)
    return {
        "forcing": gaussian(arg_keys[0], (2, 2, LEV, NLAT, NLON), 1.0, 6.0, ((3, 4), (4, 8)), jnp.float32),
        "zonal": jnp.clip(jax.random.uniform(arg_keys[1], (LEV, NLAT, NLON), jnp.float32, -0.3, 0.3) * shard_levels(arg_keys[1], (LEV, NLAT, NLON), ((1, 4), (2, 8)), -0.4, 0.0), -0.3, 0.3),
        "meridional": jnp.clip(jax.random.uniform(arg_keys[2], (LEV, NLAT, NLON), jnp.float32, -0.3, 0.3) * shard_levels(arg_keys[2], (LEV, NLAT, NLON), ((1, 4), (2, 8)), -0.4, 0.0), -0.3, 0.3),
        "mixing": jnp.clip(jnp.exp(math.log(0.24) - 2.0794415 * jax.random.uniform(arg_keys[3], (LEV - 1, NLAT, NLON), jnp.float32) ** shard_levels(arg_keys[3], (LEV - 1, NLAT, NLON), ((1, 4), (2, 8)), -0.2, 0.2)), 0.03, 0.24),
        "panel": noise_with(arg_keys[4], (ORDER, N_LAT, GCOLS), ORDER ** -0.5, 0.125, ((0, 4), (2, 8)), (0, 1, 4, 2.0)),
    }


def diffuse(tracer, mixing):
    flow = mixing * (tracer[..., 1:, :, :] - tracer[..., :-1, :, :])
    zeros = jnp.zeros_like(flow[..., :1, :, :])
    return tracer + jnp.concatenate([flow, zeros], -3) - jnp.concatenate([zeros, flow], -3)


def advect(tracer, zonal, merid_masked):
    out_east = jnp.maximum(zonal, 0.0)
    in_west = jnp.roll(jnp.minimum(zonal, 0.0), 1, -1)
    out_north = jnp.maximum(merid_masked, 0.0)
    south_min = jnp.minimum(merid_masked, 0.0)
    in_south = jnp.concatenate([jnp.zeros_like(south_min[:, :1]), south_min[:, :-1]], 1)
    east = jnp.roll(tracer, -1, -1)
    west = jnp.roll(tracer, 1, -1)
    zero_row = jnp.zeros_like(tracer[..., :1, :])
    north = jnp.concatenate([tracer[..., 1:, :], zero_row], -2)
    south = jnp.concatenate([zero_row, tracer[..., :-1, :]], -2)
    return (tracer * (1.0 - out_east + in_west - out_north + in_south)
            + east * out_east - west * in_west + north * out_north - south * in_south)


def to_blocks(values):
    leading = values.shape[:-2]
    shaped = values.reshape(leading + (NLAT // CLAT, CLAT, NLON // CLON, CLON))
    shaped = jnp.swapaxes(shaped, -3, -2)
    return shaped.reshape(leading + (ORDER,))


def reference(forcing, zonal, meridional, mixing, panel):
    top_mask = (jnp.arange(NLAT) < NLAT - 1).astype(meridional.dtype)[None, :, None]
    merid_masked = meridional * top_mask
    lam_one = advect(diffuse(forcing[1], mixing), zonal, merid_masked)
    middle = lam_one + forcing[0]
    adjoint_state = advect(diffuse(middle, mixing), zonal, merid_masked)
    surface = forcing[1][:, 0] + middle[:, 0]
    flux_vec = to_blocks(surface).astype(jnp.bfloat16)
    state_vec = to_blocks(adjoint_state).reshape(2 * LEV, ORDER).astype(jnp.bfloat16)
    vectors = jnp.concatenate([flux_vec, state_vec], 0)
    row_block = ORDER // N_LAT

    def accumulate(total, index):
        start = (index * row_block).astype(jnp.int32)
        rows_part = lax.dynamic_slice_in_dim(panel, start, row_block, 0).reshape(row_block, ORDER)
        vec_part = lax.dynamic_slice_in_dim(vectors, start, row_block, 1)
        return total + jnp.dot(vec_part, rows_part, preferred_element_type=jnp.float32), None

    total, unused = lax.scan(accumulate, jnp.zeros((2 + 2 * LEV, ORDER), jnp.float32),
                             jnp.arange(N_LAT, dtype=jnp.int32))
    total = total.reshape(2 + 2 * LEV, N_LAT, GCOLS)
    flux_grad = total[:2]
    state_grad = total[2:].reshape(2, LEV, N_LAT, GCOLS)
    return (adjoint_state, state_grad, flux_grad)
```

```python
import functools
import jax
import jax.numpy as jnp
from jax import lax
from jax.experimental import pallas as pl
from jax.experimental.pallas import tpu as pltpu
from jax.sharding import PartitionSpec as P

DIRECT = 4


def roll(value, shift, axis=-1):
    axis %= value.ndim
    return pltpu.roll(value, shift % value.shape[axis], axis)


def band_kernel(rows, cols, blocks, exchanged, band_ref, vec_ref, adjoint_ref, all_ref):
    me = lax.axis_index("lon")
    cells = rows * cols
    two = 2 * cols

    def load(block):
        if exchanged:
            apart = jnp.bitwise_xor(block, me)
            place = (apart % 2) * (blocks // 2) + apart // 2
        else:
            place = block
        return band_ref[place]

    loaded = [load(block) for block in range(blocks)]

    def field(start, count):
        return jnp.stack([block[start : start + 8 * count].reshape(count, 8, cells) for block in loaded])

    forced, first, zonal, merid, mixing, halo = (
        field(0, 2), field(16, 2), field(32, 1), field(40, 1), field(48, 1), field(56, 2))
    lane = lax.broadcasted_iota(jnp.int32, (1, 1, 8, cells), 3)
    column = lane % cols

    def tile(main, source, place):
        beyond = roll(source, two - place * 2 * two)
        return jnp.where(lane < two, roll(main, two), jnp.where(lane < 3 * two, beyond, roll(main, 3 * two)))

    def rotated(value, by):
        return jnp.concatenate([value[by:], value[:by]], 0)

    def east(value):
        return jnp.where(column == cols - 1, roll(rotated(value, 1), cols - 1), roll(value, -1))

    def west(value):
        return jnp.where(column == 0, roll(rotated(value, -1), 1 - cols), roll(value, 1))

    def north(value, edge=None):
        moved = roll(value, -cols)
        return moved if edge is None else jnp.where(lane >= cells - cols, roll(edge, -3 * cols), moved)

    def south(value, edge=None):
        moved = roll(value, cols)
        return moved if edge is None else jnp.where(lane < cols, roll(edge, -5 * cols), moved)

    def diffuse(value, mix):
        flow = mix * (roll(value, -1, -2) - value)
        return value + flow - roll(flow, 1, -2)

    def factors(across, along, edge=None):
        out_east = jnp.maximum(across, 0.0)
        in_west = jnp.minimum(west(across), 0.0)
        out_north = jnp.maximum(along, 0.0)
        in_south = jnp.minimum(south(along, edge), 0.0)
        return (1.0 - out_east + in_west - out_north + in_south, out_east, in_west, out_north, in_south)

    def advect(value, factor, edge=None):
        centre, out_east, in_west, out_north, in_south = factor
        return (value * centre + east(value) * out_east - west(value) * in_west
                + north(value, edge) * out_north - south(value, edge) * in_south)

    forced_tile = tile(forced, halo, 0)
    first_tile = tile(first, halo, 1)
    zonal_tile = tile(zonal, halo[:, :1], 2)
    mixing_tile = tile(mixing, halo[:, 1:], 2)
    merid_tile = tile(merid, halo[:, :1], 3)
    main_factor = factors(zonal, merid, merid_tile)
    tile_factor = factors(zonal_tile, merid_tile)
    started = diffuse(forced, mixing)
    started_tile = diffuse(forced_tile, mixing_tile)
    middle = advect(started, main_factor, started_tile) + first
    middle_tile = advect(started_tile, tile_factor) + first_tile
    mixed = diffuse(middle, mixing)
    mixed_tile = diffuse(middle_tile, mixing_tile)
    adjoint = advect(mixed, main_factor, mixed_tile)
    surface = forced + middle
    for block in range(blocks):
        span = slice(block * cells, (block + 1) * cells)
        own = adjoint[block].reshape(16, cells)
        all_ref[block] = own
        vec_ref[:16, span] = own.astype(jnp.bfloat16)
        pair = jnp.concatenate([surface[block, 0, :1], surface[block, 1, :1]], 0)
        vec_ref[16:18, span] = pair.astype(jnp.bfloat16)
    adjoint_ref[...] = all_ref[me]


def band_vectors(band, rows, cols, blocks, exchanged):
    cells = rows * cols
    return pl.pallas_call(
        functools.partial(band_kernel, rows, cols, blocks, exchanged),
        out_shape=(jax.ShapeDtypeStruct((18, blocks * cells), jnp.bfloat16), jax.ShapeDtypeStruct((16, cells), jnp.float32)),
        in_specs=[pl.BlockSpec(memory_space=pltpu.VMEM)],
        out_specs=(pl.BlockSpec(memory_space=pltpu.VMEM), pl.BlockSpec(memory_space=pltpu.VMEM)),
        scratch_shapes=[pltpu.VMEM((blocks, 16, cells), jnp.float32)],
        name="band",
    )(band)


def swapped(value, axis, apart):
    peers = lax.axis_size(axis)
    return lax.ppermute(value, axis, [(i, i ^ apart) for i in range(peers) if i ^ apart < peers])


def along_lat(upper, lower):
    peers = lax.axis_size("lat")
    even = lax.axis_index("lat") % 2 == 0
    pairs = [(i, i ^ 1) for i in range(peers)]
    others = [(i, i + 1 if i % 2 else i - 1) for i in range(1, peers - 1)]
    nearer = lax.ppermute(jnp.where(even, upper, lower), "lat", pairs)
    farther = lax.ppermute(jnp.where(even, lower, upper), "lat", others)
    return nearer + farther


def gathered(packed):
    peers = lax.axis_size("lon")
    if peers > 2 * DIRECT:
        return lax.all_gather(packed, "lon", axis=0), False
    pieces = [packed] + [swapped(packed, "lon", apart) for apart in range(2, peers, 2)]
    own = jnp.stack(pieces)
    return jnp.concatenate([own, swapped(own, "lon", 1)], 0), True


def scattered(total):
    peers = lax.axis_size("lat")
    if peers > DIRECT:
        return lax.psum_scatter(total, "lat", scatter_dimension=1, tiled=True)
    me = lax.axis_index("lat")
    kept = lax.dynamic_slice_in_dim(total, me, 1, 1)
    for apart in range(1, peers):
        piece = lax.dynamic_slice_in_dim(total, me ^ apart, 1, 1)
        kept = kept + swapped(piece, "lat", apart)
    return kept


def shards(forcing, zonal, meridional, mixing, panel):
    levels, rows, cols = zonal.shape
    cells = rows * cols
    row_index = lax.axis_index("lat") * rows + jnp.arange(rows, dtype=jnp.int32)
    below_top = row_index < rows * lax.axis_size("lat") - 1
    masked = jnp.where(below_top[None, :, None], meridional, 0.0)
    forced = forcing[1].reshape(2 * levels, cells)
    first = forcing[0].reshape(2 * levels, cells)
    across = zonal.reshape(levels, cells)
    along = masked.reshape(levels, cells)
    mixed = jnp.concatenate([mixing.reshape(levels - 1, cells), jnp.zeros((1, cells), jnp.float32)], 0)
    pair = jnp.concatenate([across, mixed], 0)
    lone = jnp.concatenate([along, jnp.zeros_like(along)], 0)
    two = 2 * cols
    blank = jnp.zeros((2 * levels, two), jnp.float32)
    sources = (forced, first, pair, lone)
    upper = jnp.concatenate([piece for s in sources for piece in (blank, s[:, cells - two :])], 1)
    lower = jnp.concatenate([piece for s in sources for piece in (s[:, :two], blank)], 1)
    halo = along_lat(upper, lower)
    packed = jnp.concatenate([forced, first, across, along, mixed, halo], 0)
    band, exchanged = gathered(packed)
    vectors, adjoint = band_vectors(band, rows, cols, lax.axis_size("lon"), exchanged)
    total = jnp.einsum("rc,cam->ram", vectors, panel, preferred_element_type=jnp.float32)
    summed = scattered(total)
    state_grad = summed[:16].reshape(2, levels, 1, summed.shape[2])
    flux_grad = summed[16:]
    return (adjoint.reshape(2, levels, rows, cols), state_grad, flux_grad)


def solution(mesh):
    return jax.shard_map(
        shards,
        mesh=mesh,
        in_specs=(
            P(None, None, None, "lat", "lon"),
            P(None, "lat", "lon"),
            P(None, "lat", "lon"),
            P(None, "lat", "lon"),
            P("lat", None, "lon"),
        ),
        out_specs=(P(None, None, "lat", "lon"), P(None, None, "lat", "lon"), P(None, "lat", "lon")),
        check_vma=False,
    )
```

```python
import functools
import jax
import jax.numpy as jnp
from jax import lax
from jax.experimental import pallas as pl
from jax.experimental.pallas import tpu as pltpu
from jax.sharding import PartitionSpec as P


DIRECT = 4
GRANT = 4 << 20


def roll(value, shift, axis=-1):
    axis %= value.ndim
    return pltpu.roll(value, shift % value.shape[axis], axis)


def pack_kernel(rows, cols, forcing_hbm, zonal_hbm, merid_hbm, mixing_hbm, main_ref, near_ref, far_ref,
                forcing_ref, zonal_ref, merid_ref, mixing_ref, sems):
    copies = [
        pltpu.make_async_copy(source, target, sems.at[i])
        for i, (source, target) in enumerate(
            ((forcing_hbm, forcing_ref), (zonal_hbm, zonal_ref), (merid_hbm, merid_ref), (mixing_hbm, mixing_ref)))
    ]
    for copy in copies:
        copy.start()
    cells = rows * cols
    two = 2 * cols
    lane = lax.broadcasted_iota(jnp.int32, (2, 8, cells), 2)
    level = lax.broadcasted_iota(jnp.int32, (2, 8, cells), 1)
    half = lax.broadcasted_iota(jnp.int32, (2, 8, cells), 0)
    group = lane // cols
    plane = half * 8 + level

    def flat(planes):
        value = planes.reshape(16 * cols, rows).T.reshape(2, 8, cells)
        for step in (1, 2, 4):
            upper = roll(roll(value, -step, 1), step * cols)
            lower = roll(roll(value, step, 1), -step * cols)
            here, there = (plane // step) % 2, (group // step) % 2
            value = jnp.where(here == there, value, jnp.where(here == 0, upper, lower))
        crossed = jnp.concatenate([value[1:], value[:1]], 0)
        crossed = roll(crossed, 8 * cols)
        return jnp.where(half == group // 8, value, crossed)

    copies[0].wait()
    forced = flat(forcing_ref[1].reshape(16, cols, rows))
    first = flat(forcing_ref[0].reshape(16, cols, rows))
    copies[1].wait()
    copies[3].wait()
    pair = flat(jnp.concatenate([zonal_ref[...], mixing_ref[...], jnp.zeros((1, cols, rows), jnp.float32)], 0))
    copies[2].wait()
    merid = merid_ref[...]
    lone = flat(jnp.concatenate([merid, jnp.zeros_like(merid)], 0))
    place = lax.axis_index("lat")
    top = jnp.where(place == lax.axis_size("lat") - 1, 1, 0)
    lone = jnp.where((group == rows - 1) & (top == 1), 0.0, lone)
    main_ref[0:16] = forced.reshape(16, cells)
    main_ref[16:32] = first.reshape(16, cells)
    main_ref[32:48] = pair.reshape(16, cells)
    main_ref[48:56] = lone[0]
    upper = jnp.zeros((2, 8, cells), jnp.float32)
    lower = jnp.zeros((2, 8, cells), jnp.float32)
    for i, value in enumerate((forced, first, pair, lone)):
        start = 2 * two * i
        lower = jnp.where((lane >= start) & (lane < start + two), roll(value, start), lower)
        upper = jnp.where((lane >= start + two) & (lane < start + 2 * two), roll(value, start + 2 * two), upper)
    even = jnp.where(place % 2 == 0, 1, 0)
    mine = jnp.broadcast_to(even, upper.shape) == 1
    near_ref[...] = jnp.where(mine, upper, lower).reshape(16, cells)
    far_ref[...] = jnp.where(mine, lower, upper).reshape(16, cells)


def packed_fields(forcing, zonal, meridional, mixing):
    _, rows, cols = zonal.shape
    cells = rows * cols
    fields = (forcing, zonal, meridional, mixing)
    values = [pltpu.with_memory_space_constraint(jnp.swapaxes(v, -1, -2), pltpu.HBM) for v in fields]
    edge = jax.ShapeDtypeStruct((16, cells), jnp.float32)
    return pl.pallas_call(
        functools.partial(pack_kernel, rows, cols),
        out_shape=(jax.ShapeDtypeStruct((56, cells), jnp.float32), edge, edge),
        in_specs=[pl.BlockSpec(memory_space=pltpu.HBM)] * 4,
        out_specs=[pl.BlockSpec(memory_space=pltpu.VMEM)] * 3,
        scratch_shapes=[pltpu.VMEM(v.shape, jnp.float32) for v in values] + [pltpu.SemaphoreType.DMA((4,))],
        compiler_params=pltpu.CompilerParams(vmem_limit_bytes=GRANT),
        name="pack",
    )(*values)


def band_kernel(rows, cols, blocks, exchanged, *refs):
    *band_refs, vec_ref, adjoint_ref, all_ref = refs
    me = lax.axis_index("lon")
    cells = rows * cols
    two = 2 * cols
    if exchanged:
        same, other = band_refs
        odd = jnp.broadcast_to(me % 2, (72, cells)) == 1
        loaded = []
        for chip in range(blocks // 2):
            place = jnp.bitwise_xor(chip, me // 2)
            here, there = same[place], other[place]
            loaded += [jnp.where(odd, there, here), jnp.where(odd, here, there)]
    else:
        loaded = [band_refs[0][block] for block in range(blocks)]

    def field(start, count):
        return jnp.stack([block[start : start + 8 * count].reshape(count, 8, cells) for block in loaded])

    forced, first, zonal, merid, mixing, halo = (
        field(0, 2), field(16, 2), field(32, 1), field(48, 1), field(40, 1), field(56, 2))
    lane = lax.broadcasted_iota(jnp.int32, (1, 1, 8, cells), 3)
    column = lane % cols

    def tile(main, source, place):
        beyond = roll(source, two - place * 2 * two)
        return jnp.where(lane < two, roll(main, two), jnp.where(lane < 3 * two, beyond, roll(main, 3 * two)))

    def rotated(value, by):
        return jnp.concatenate([value[by:], value[:by]], 0)

    def east(value):
        return jnp.where(column == cols - 1, roll(rotated(value, 1), cols - 1), roll(value, -1))

    def west(value):
        return jnp.where(column == 0, roll(rotated(value, -1), 1 - cols), roll(value, 1))

    def north(value, edge=None):
        moved = roll(value, -cols)
        return moved if edge is None else jnp.where(lane >= cells - cols, roll(edge, -3 * cols), moved)

    def south(value, edge=None):
        moved = roll(value, cols)
        return moved if edge is None else jnp.where(lane < cols, roll(edge, -5 * cols), moved)

    def diffuse(value, mix):
        flow = mix * (roll(value, -1, -2) - value)
        return value + flow - roll(flow, 1, -2)

    def factors(across, along, edge=None):
        out_east = jnp.maximum(across, 0.0)
        in_west = jnp.minimum(west(across), 0.0)
        out_north = jnp.maximum(along, 0.0)
        in_south = jnp.minimum(south(along, edge), 0.0)
        return (1.0 - out_east + in_west - out_north + in_south, out_east, in_west, out_north, in_south)

    def advect(value, factor, edge=None):
        centre, out_east, in_west, out_north, in_south = factor
        return (value * centre + east(value) * out_east - west(value) * in_west
                + north(value, edge) * out_north - south(value, edge) * in_south)

    forced_tile = tile(forced, halo, 0)
    first_tile = tile(first, halo, 1)
    zonal_tile = tile(zonal, halo[:, :1], 2)
    mixing_tile = tile(mixing, halo[:, 1:], 2)
    merid_tile = tile(merid, halo[:, :1], 3)
    main_factor = factors(zonal, merid, merid_tile)
    tile_factor = factors(zonal_tile, merid_tile)
    started = diffuse(forced, mixing)
    started_tile = diffuse(forced_tile, mixing_tile)
    middle = advect(started, main_factor, started_tile) + first
    middle_tile = advect(started_tile, tile_factor) + first_tile
    mixed = diffuse(middle, mixing)
    mixed_tile = diffuse(middle_tile, mixing_tile)
    adjoint = advect(mixed, main_factor, mixed_tile)
    surface = forced + middle
    for block in range(blocks):
        span = slice(block * cells, (block + 1) * cells)
        own = adjoint[block].reshape(16, cells)
        all_ref[block] = own
        vec_ref[:16, span] = own.astype(jnp.bfloat16)
        pair = jnp.concatenate([surface[block, 0, :1], surface[block, 1, :1]], 0)
        vec_ref[16:18, span] = pair.astype(jnp.bfloat16)
    adjoint_ref[...] = all_ref[me]


def band_vectors(band, rows, cols, blocks, exchanged):
    cells = rows * cols
    return pl.pallas_call(
        functools.partial(band_kernel, rows, cols, blocks, exchanged),
        out_shape=(jax.ShapeDtypeStruct((18, blocks * cells), jnp.bfloat16), jax.ShapeDtypeStruct((16, cells), jnp.float32)),
        in_specs=[pl.BlockSpec(memory_space=pltpu.VMEM)] * len(band),
        out_specs=(pl.BlockSpec(memory_space=pltpu.VMEM), pl.BlockSpec(memory_space=pltpu.VMEM)),
        scratch_shapes=[pltpu.VMEM((blocks, 16, cells), jnp.float32)],
        compiler_params=pltpu.CompilerParams(vmem_limit_bytes=GRANT * (1 if exchanged else 4)),
        name="band",
    )(*band)


def swapped(value, axis, apart):
    peers = lax.axis_size(axis)
    return lax.ppermute(value, axis, [(i, i ^ apart) for i in range(peers) if i ^ apart < peers])


def along_lat(nearer, farther):
    peers = lax.axis_size("lat")
    others = [(i, i + 1 if i % 2 else i - 1) for i in range(1, peers - 1)]
    farther = lax.ppermute(farther, "lat", others)
    nearer = swapped(nearer, "lat", 1)
    return nearer + farther


def gathered(packed):
    peers = lax.axis_size("lon")
    if peers > 2 * DIRECT:
        return (lax.all_gather(packed, "lon", axis=0),), False
    pieces = [packed]
    for apart in range(2, peers, 2):
        pieces.append(swapped(packed, "lon", apart))
    same = jnp.stack(pieces)
    return (same, swapped(same, "lon", 1)), True


def scattered(total):
    peers = lax.axis_size("lat")
    if peers > DIRECT:
        return lax.psum_scatter(total, "lat", scatter_dimension=1, tiled=True)
    me = lax.axis_index("lat")
    kept = lax.dynamic_slice_in_dim(total, me, 1, 1)
    for apart in range(1, peers):
        piece = lax.dynamic_slice_in_dim(total, me ^ apart, 1, 1)
        kept = kept + swapped(piece, "lat", apart)
    return kept


def shards(forcing, zonal, meridional, mixing, panel):
    levels, rows, cols = zonal.shape
    main, nearer, farther = packed_fields(forcing, zonal, meridional, mixing)
    packed = jnp.concatenate([main, along_lat(nearer, farther)], 0)
    band, exchanged = gathered(packed)
    vectors, adjoint = band_vectors(band, rows, cols, lax.axis_size("lon"), exchanged)
    total = jnp.einsum("rc,cam->ram", vectors, panel, preferred_element_type=jnp.float32)
    summed = scattered(total)
    state_grad = summed[:16].reshape(2, levels, 1, summed.shape[2])
    flux_grad = summed[16:]
    return (adjoint.reshape(2, levels, rows, cols), state_grad, flux_grad)


def solution(mesh):
    return jax.shard_map(
        shards,
        mesh=mesh,
        in_specs=(
            P(None, None, None, "lat", "lon"),
            P(None, "lat", "lon"),
            P(None, "lat", "lon"),
            P(None, "lat", "lon"),
            P("lat", None, "lon"),
        ),
        out_specs=(P(None, None, "lat", "lon"), P(None, None, "lat", "lon"), P(None, "lat", "lon")),
        check_vma=False,
    )
```

```python
import functools
import jax
import jax.numpy as jnp
from jax import lax
from jax.experimental import pallas as pl
from jax.experimental.pallas import tpu as pltpu
from jax.sharding import PartitionSpec as P


DIRECT = 4
GRANT = 4 << 20
EDGE_CROSS = 1
CHIP_CROSS = 1


def roll(value, shift, axis=-1):
    axis %= value.ndim
    return pltpu.roll(value, shift % value.shape[axis], axis)


def pack_kernel(rows, cols, forcing_hbm, zonal_hbm, merid_hbm, mixing_hbm, main_ref, near_ref, far_ref,
                forcing_ref, zonal_ref, merid_ref, mixing_ref, sems):
    copies = [
        pltpu.make_async_copy(source, target, sems.at[i])
        for i, (source, target) in enumerate(
            ((forcing_hbm, forcing_ref), (zonal_hbm, zonal_ref), (merid_hbm, merid_ref), (mixing_hbm, mixing_ref)))
    ]
    for copy in copies:
        copy.start()
    cells = rows * cols
    two = 2 * cols
    lane = lax.broadcasted_iota(jnp.int32, (2, 8, cells), 2)
    level = lax.broadcasted_iota(jnp.int32, (2, 8, cells), 1)
    half = lax.broadcasted_iota(jnp.int32, (2, 8, cells), 0)
    group = lane // cols
    plane = half * 8 + level

    def flat(planes):
        value = planes.reshape(16 * cols, rows).T.reshape(2, 8, cells)
        for step in (1, 2, 4):
            upper = roll(roll(value, -step, 1), step * cols)
            lower = roll(roll(value, step, 1), -step * cols)
            here, there = (plane // step) % 2, (group // step) % 2
            value = jnp.where(here == there, value, jnp.where(here == 0, upper, lower))
        crossed = jnp.concatenate([value[1:], value[:1]], 0)
        crossed = roll(crossed, 8 * cols)
        return jnp.where(half == group // 8, value, crossed)

    copies[0].wait()
    forced = flat(forcing_ref[1].reshape(16, cols, rows))
    first = flat(forcing_ref[0].reshape(16, cols, rows))
    copies[1].wait()
    copies[3].wait()
    pair = flat(jnp.concatenate([zonal_ref[...], mixing_ref[...], jnp.zeros((1, cols, rows), jnp.float32)], 0))
    copies[2].wait()
    merid = merid_ref[...]
    lone = flat(jnp.concatenate([merid, jnp.zeros_like(merid)], 0))
    place = lax.axis_index("lat")
    top = jnp.where(place == lax.axis_size("lat") - 1, 1, 0)
    lone = jnp.where((group == rows - 1) & (top == 1), 0.0, lone)
    main_ref[0:16] = forced.reshape(16, cells)
    main_ref[16:32] = first.reshape(16, cells)
    main_ref[32:48] = pair.reshape(16, cells)
    main_ref[48:56] = lone[0]
    upper = jnp.zeros((2, 8, cells), jnp.float32)
    lower = jnp.zeros((2, 8, cells), jnp.float32)
    for i, value in enumerate((forced, first, pair, lone)):
        start = 2 * two * i
        lower = jnp.where((lane >= start) & (lane < start + two), roll(value, start), lower)
        upper = jnp.where((lane >= start + two) & (lane < start + 2 * two), roll(value, start + 2 * two), upper)
    even = place % 2 == 0
    near_ref[...] = jnp.where(even, upper, lower).reshape(16, cells)
    ended = (place == 0) | ((place == lax.axis_size("lat") - 1) & ~even)
    far_ref[...] = jnp.where(ended, 0.0, jnp.where(even, lower, upper)).reshape(16, cells)


def packed_fields(forcing, zonal, meridional, mixing):
    _, rows, cols = zonal.shape
    cells = rows * cols
    fields = (forcing, zonal, meridional, mixing)
    values = [pltpu.with_memory_space_constraint(jnp.swapaxes(v, -1, -2), pltpu.HBM) for v in fields]
    edge = jax.ShapeDtypeStruct((16, cells), jnp.float32)
    return pl.pallas_call(
        functools.partial(pack_kernel, rows, cols),
        out_shape=(jax.ShapeDtypeStruct((56, cells), jnp.float32), edge, edge),
        in_specs=[pl.BlockSpec(memory_space=pltpu.HBM)] * 4,
        out_specs=[pl.BlockSpec(memory_space=pltpu.VMEM)] * 3,
        scratch_shapes=[pltpu.VMEM(v.shape, jnp.float32) for v in values] + [pltpu.SemaphoreType.DMA((4,))],
        compiler_params=pltpu.CompilerParams(vmem_limit_bytes=GRANT),
        name="pack",
    )(*values)


def band_kernel(rows, cols, blocks, exchanged, *refs):
    *band_refs, vec_ref, adjoint_ref, all_ref = refs
    me = lax.axis_index("lon")
    cells = rows * cols
    two = 2 * cols
    mains, halos = [], []
    if exchanged:
        same, other = band_refs
        for chip in range(blocks // 2):
            place = jnp.bitwise_xor(chip, me // 2)
            turned = (me + CHIP_CROSS * jnp.where(place == 0, 0, 1)) % 2 == 1
            here, there = same[place], other[place]
            pair = [jnp.where(turned, there, here), jnp.where(turned, here, there)]
            mains += [piece[:56] for piece in pair]
            halos += [piece[56:] for piece in (pair[::-1] if EDGE_CROSS else pair)]
    else:
        mains = [band_refs[0][block, :56] for block in range(blocks)]
        halos = [band_refs[0][block ^ EDGE_CROSS, 56:] for block in range(blocks)]

    def field(start, count):
        return jnp.stack([block[start : start + 8 * count].reshape(count, 8, cells) for block in mains])

    forced, first, zonal, merid, mixing = field(0, 2), field(16, 2), field(32, 1), field(48, 1), field(40, 1)
    halo = jnp.stack([block.reshape(2, 8, cells) for block in halos])
    lane = lax.broadcasted_iota(jnp.int32, (1, 1, 8, cells), 3)
    column = lane % cols

    def tile(main, source, place):
        beyond = roll(source, two - place * 2 * two)
        return jnp.where(lane < two, roll(main, two), jnp.where(lane < 3 * two, beyond, roll(main, 3 * two)))

    def rotated(value, by):
        return jnp.concatenate([value[by:], value[:by]], 0)

    def east(value):
        return jnp.where(column == cols - 1, roll(rotated(value, 1), cols - 1), roll(value, -1))

    def west(value):
        return jnp.where(column == 0, roll(rotated(value, -1), 1 - cols), roll(value, 1))

    def north(value, edge=None):
        moved = roll(value, -cols)
        return moved if edge is None else jnp.where(lane >= cells - cols, roll(edge, -3 * cols), moved)

    def south(value, edge=None):
        moved = roll(value, cols)
        return moved if edge is None else jnp.where(lane < cols, roll(edge, -5 * cols), moved)

    def diffuse(value, mix):
        flow = mix * (roll(value, -1, -2) - value)
        return value + flow - roll(flow, 1, -2)

    def factors(across, along, edge=None):
        out_east = jnp.maximum(across, 0.0)
        in_west = jnp.minimum(west(across), 0.0)
        out_north = jnp.maximum(along, 0.0)
        in_south = jnp.minimum(south(along, edge), 0.0)
        return (1.0 - out_east + in_west - out_north + in_south, out_east, in_west, out_north, in_south)

    def advect(value, factor, edge=None):
        centre, out_east, in_west, out_north, in_south = factor
        return (value * centre + east(value) * out_east - west(value) * in_west
                + north(value, edge) * out_north - south(value, edge) * in_south)

    forced_tile = tile(forced, halo, 0)
    first_tile = tile(first, halo, 1)
    zonal_tile = tile(zonal, halo[:, :1], 2)
    mixing_tile = tile(mixing, halo[:, 1:], 2)
    merid_tile = tile(merid, halo[:, :1], 3)
    main_factor = factors(zonal, merid, merid_tile)
    tile_factor = factors(zonal_tile, merid_tile)
    started = diffuse(forced, mixing)
    started_tile = diffuse(forced_tile, mixing_tile)
    middle = advect(started, main_factor, started_tile) + first
    middle_tile = advect(started_tile, tile_factor) + first_tile
    mixed = diffuse(middle, mixing)
    mixed_tile = diffuse(middle_tile, mixing_tile)
    adjoint = advect(mixed, main_factor, mixed_tile)
    surface = forced + middle
    for block in range(blocks):
        span = slice(block * cells, (block + 1) * cells)
        own = adjoint[block].reshape(16, cells)
        all_ref[block] = own
        vec_ref[:16, span] = own.astype(jnp.bfloat16)
        pair = jnp.concatenate([surface[block, 0, :1], surface[block, 1, :1]], 0)
        vec_ref[16:18, span] = pair.astype(jnp.bfloat16)
    adjoint_ref[...] = all_ref[me]


def band_vectors(band, rows, cols, blocks, exchanged):
    cells = rows * cols
    return pl.pallas_call(
        functools.partial(band_kernel, rows, cols, blocks, exchanged),
        out_shape=(jax.ShapeDtypeStruct((18, blocks * cells), jnp.bfloat16), jax.ShapeDtypeStruct((16, cells), jnp.float32)),
        in_specs=[pl.BlockSpec(memory_space=pltpu.VMEM)] * len(band),
        out_specs=(pl.BlockSpec(memory_space=pltpu.VMEM), pl.BlockSpec(memory_space=pltpu.VMEM)),
        scratch_shapes=[pltpu.VMEM((blocks, 16, cells), jnp.float32)],
        compiler_params=pltpu.CompilerParams(vmem_limit_bytes=GRANT * (1 if exchanged else 4)),
        name="band",
    )(*band)


def moved(value, target):
    lats, lons = lax.axis_size("lat"), lax.axis_size("lon")
    pairs = []
    for lat in range(lats):
        for lon in range(lons):
            to_lat, to_lon = target(lat, lon)
            pairs.append((lat * lons + lon, to_lat % lats * lons + to_lon))
    return lax.ppermute(value, ("lat", "lon"), pairs)


def along_lat(nearer, farther):
    farther = moved(farther, lambda lat, lon: (lat + 1 if lat % 2 else lat - 1, lon ^ EDGE_CROSS))
    nearer = moved(nearer, lambda lat, lon: (lat ^ 1, lon ^ EDGE_CROSS))
    return nearer + farther


def gathered(packed):
    peers = lax.axis_size("lon")
    if peers > 2 * DIRECT:
        return (lax.all_gather(packed, "lon", axis=0),), False
    pieces = [packed]
    for apart in range(2, peers, 2):
        pieces.append(moved(packed, lambda lat, lon: (lat, lon ^ apart ^ CHIP_CROSS)))
    same = jnp.stack(pieces)
    return (same, moved(same, lambda lat, lon: (lat, lon ^ 1))), True


def sum_kernel(own_ref, *refs):
    *piece_refs, state_hbm, flux_hbm, state_ref, flux_ref, sems = refs
    value = own_ref[0]
    for piece_ref in piece_refs:
        value = value + piece_ref[0]
    rows = state_ref.shape[0] * state_ref.shape[1]
    state_ref[...] = value[:rows].reshape(state_ref.shape)
    flux_ref[...] = value[rows:].reshape(flux_ref.shape)
    copies = [pltpu.make_async_copy(state_ref, state_hbm, sems.at[0]), pltpu.make_async_copy(flux_ref, flux_hbm, sems.at[1])]
    for copy in copies:
        copy.start()
    for copy in copies:
        copy.wait()


def scattered(total, levels):
    peers, _, columns = total.shape
    shapes = ((2, levels, 1, columns), (2, 1, columns))
    if peers > DIRECT:
        value = lax.psum_scatter(total, "lat", scatter_dimension=0, tiled=True)[0]
        return value[:16].reshape(shapes[0]), value[16:].reshape(shapes[1])
    me = lax.axis_index("lat")
    pieces = [lax.dynamic_slice_in_dim(total, me, 1, 0)]
    for apart in range(1, peers):
        piece = lax.dynamic_slice_in_dim(total, me ^ apart, 1, 0)
        pieces.append(moved(piece, lambda lat, lon: (lat ^ apart, lon)))
    return pl.pallas_call(
        sum_kernel,
        out_shape=[jax.ShapeDtypeStruct(shape, jnp.float32) for shape in shapes],
        in_specs=[pl.BlockSpec(memory_space=pltpu.VMEM)] * peers,
        out_specs=[pl.BlockSpec(memory_space=pltpu.HBM)] * 2,
        scratch_shapes=[pltpu.VMEM(shape, jnp.float32) for shape in shapes] + [pltpu.SemaphoreType.DMA((2,))],
        compiler_params=pltpu.CompilerParams(vmem_limit_bytes=GRANT),
        name="total",
    )(*pieces)


def shards(forcing, zonal, meridional, mixing, panel):
    levels, rows, cols = zonal.shape
    main, nearer, farther = packed_fields(forcing, zonal, meridional, mixing)
    packed = jnp.concatenate([main, along_lat(nearer, farther)], 0)
    band, exchanged = gathered(packed)
    vectors, adjoint = band_vectors(band, rows, cols, lax.axis_size("lon"), exchanged)
    total = jnp.einsum("rc,cam->arm", vectors, panel, preferred_element_type=jnp.float32)
    state_grad, flux_grad = scattered(total, levels)
    return (adjoint.reshape(2, levels, rows, cols), state_grad, flux_grad)


def solution(mesh):
    return jax.shard_map(
        shards,
        mesh=mesh,
        in_specs=(
            P(None, None, None, "lat", "lon"),
            P(None, "lat", "lon"),
            P(None, "lat", "lon"),
            P(None, "lat", "lon"),
            P("lat", None, "lon"),
        ),
        out_specs=(P(None, None, "lat", "lon"), P(None, None, "lat", "lon"), P(None, "lat", "lon")),
        check_vma=False,
    )
```

```python
import functools
import jax
import jax.numpy as jnp
from jax import lax
from jax.experimental import pallas as pl
from jax.experimental.layout import Layout, with_layout_constraint
from jax.experimental.pallas import tpu as pltpu
from jax.sharding import PartitionSpec as P


DIRECT = 4
GRANT = 4 << 20
EDGE_CROSS = 1
CHIP_CROSS = 1
EARLY = (4,)


def roll(value, shift, axis=-1):
    axis %= value.ndim
    return pltpu.roll(value, shift % value.shape[axis], axis)


def pack_kernel(rows, cols, forcing_hbm, zonal_hbm, merid_hbm, mixing_hbm, main_ref, near_ref, far_ref,
                forcing_ref, zonal_ref, merid_ref, mixing_ref, sems):
    copies = [
        pltpu.make_async_copy(source, target, sems.at[i])
        for i, (source, target) in enumerate(
            ((forcing_hbm, forcing_ref), (zonal_hbm, zonal_ref), (merid_hbm, merid_ref), (mixing_hbm, mixing_ref)))
    ]
    for copy in copies:
        copy.start()
    cells = rows * cols
    two = 2 * cols
    lane = lax.broadcasted_iota(jnp.int32, (2, 8, cells), 2)
    level = lax.broadcasted_iota(jnp.int32, (2, 8, cells), 1)
    half = lax.broadcasted_iota(jnp.int32, (2, 8, cells), 0)
    group = lane // cols
    plane = half * 8 + level

    def flat(planes):
        value = planes.reshape(16 * cols, rows).T.reshape(2, 8, cells)
        for step in (1, 2, 4):
            upper = roll(roll(value, -step, 1), step * cols)
            lower = roll(roll(value, step, 1), -step * cols)
            here, there = (plane // step) % 2, (group // step) % 2
            value = jnp.where(here == there, value, jnp.where(here == 0, upper, lower))
        crossed = jnp.concatenate([value[1:], value[:1]], 0)
        crossed = roll(crossed, 8 * cols)
        return jnp.where(half == group // 8, value, crossed)

    copies[0].wait()
    forced = flat(forcing_ref[1].reshape(16, cols, rows))
    first = flat(forcing_ref[0].reshape(16, cols, rows))
    copies[1].wait()
    copies[3].wait()
    pair = flat(jnp.concatenate([zonal_ref[...], mixing_ref[...], jnp.zeros((1, cols, rows), jnp.float32)], 0))
    copies[2].wait()
    merid = merid_ref[...]
    lone = flat(jnp.concatenate([merid, jnp.zeros_like(merid)], 0))
    place = lax.axis_index("lat")
    top = jnp.where(place == lax.axis_size("lat") - 1, 1, 0)
    lone = jnp.where((group == rows - 1) & (top == 1), 0.0, lone)
    main_ref[0:16] = forced.reshape(16, cells)
    main_ref[16:32] = first.reshape(16, cells)
    main_ref[32:48] = pair.reshape(16, cells)
    main_ref[48:56] = lone[0]
    upper = jnp.zeros((2, 8, cells), jnp.float32)
    lower = jnp.zeros((2, 8, cells), jnp.float32)
    for i, value in enumerate((forced, first, pair, lone)):
        start = 2 * two * i
        lower = jnp.where((lane >= start) & (lane < start + two), roll(value, start), lower)
        upper = jnp.where((lane >= start + two) & (lane < start + 2 * two), roll(value, start + 2 * two), upper)
    even = place % 2 == 0
    near_ref[...] = jnp.where(even, upper, lower).reshape(16, cells)
    ended = (place == 0) | ((place == lax.axis_size("lat") - 1) & ~even)
    far_ref[...] = jnp.where(ended, 0.0, jnp.where(even, lower, upper)).reshape(16, cells)


def packed_fields(forcing, zonal, meridional, mixing):
    _, rows, cols = zonal.shape
    cells = rows * cols
    fields = (forcing, zonal, meridional, mixing)
    values = [pltpu.with_memory_space_constraint(jnp.swapaxes(v, -1, -2), pltpu.HBM) for v in fields]
    edge = jax.ShapeDtypeStruct((16, cells), jnp.float32)
    return pl.pallas_call(
        functools.partial(pack_kernel, rows, cols),
        out_shape=(jax.ShapeDtypeStruct((56, cells), jnp.float32), edge, edge),
        in_specs=[pl.BlockSpec(memory_space=pltpu.HBM)] * 4,
        out_specs=[pl.BlockSpec(memory_space=pltpu.VMEM)] * 3,
        scratch_shapes=[pltpu.VMEM(v.shape, jnp.float32) for v in values] + [pltpu.SemaphoreType.DMA((4,))],
        compiler_params=pltpu.CompilerParams(vmem_limit_bytes=GRANT),
        name="pack",
    )(*values)


def band_kernel(rows, cols, blocks, exchanged, *refs):
    *band_refs, vec_ref, adjoint_ref, all_ref = refs
    me = lax.axis_index("lon")
    cells = rows * cols
    two = 2 * cols
    mains, halos = [], []
    if exchanged:
        same, other = band_refs
        for chip in range(blocks // 2):
            place = jnp.bitwise_xor(chip, me // 2)
            turned = (me + CHIP_CROSS * jnp.where(place == 0, 0, 1)) % 2 == 1
            here, there = same[place], other[place]
            pair = [jnp.where(turned, there, here), jnp.where(turned, here, there)]
            mains += [piece[:56] for piece in pair]
            halos += [piece[56:] for piece in (pair[::-1] if EDGE_CROSS else pair)]
    else:
        mains = [band_refs[0][block, :56] for block in range(blocks)]
        halos = [band_refs[0][block ^ EDGE_CROSS, 56:] for block in range(blocks)]

    def field(start, count):
        return jnp.stack([block[start : start + 8 * count].reshape(count, 8, cells) for block in mains])

    forced, first, zonal, merid, mixing = field(0, 2), field(16, 2), field(32, 1), field(48, 1), field(40, 1)
    halo = jnp.stack([block.reshape(2, 8, cells) for block in halos])
    lane = lax.broadcasted_iota(jnp.int32, (1, 1, 8, cells), 3)
    column = lane % cols

    def tile(main, source, place):
        beyond = roll(source, two - place * 2 * two)
        return jnp.where(lane < two, roll(main, two), jnp.where(lane < 3 * two, beyond, roll(main, 3 * two)))

    def rotated(value, by):
        return jnp.concatenate([value[by:], value[:by]], 0)

    def east(value):
        return jnp.where(column == cols - 1, roll(rotated(value, 1), cols - 1), roll(value, -1))

    def west(value):
        return jnp.where(column == 0, roll(rotated(value, -1), 1 - cols), roll(value, 1))

    def north(value, edge=None):
        moved = roll(value, -cols)
        return moved if edge is None else jnp.where(lane >= cells - cols, roll(edge, -3 * cols), moved)

    def south(value, edge=None):
        moved = roll(value, cols)
        return moved if edge is None else jnp.where(lane < cols, roll(edge, -5 * cols), moved)

    def diffuse(value, mix):
        flow = mix * (roll(value, -1, -2) - value)
        return value + flow - roll(flow, 1, -2)

    def factors(across, along, edge=None):
        out_east = jnp.maximum(across, 0.0)
        in_west = jnp.minimum(west(across), 0.0)
        out_north = jnp.maximum(along, 0.0)
        in_south = jnp.minimum(south(along, edge), 0.0)
        return (1.0 - out_east + in_west - out_north + in_south, out_east, in_west, out_north, in_south)

    def advect(value, factor, edge=None):
        centre, out_east, in_west, out_north, in_south = factor
        return (value * centre + east(value) * out_east - west(value) * in_west
                + north(value, edge) * out_north - south(value, edge) * in_south)

    forced_tile = tile(forced, halo, 0)
    first_tile = tile(first, halo, 1)
    zonal_tile = tile(zonal, halo[:, :1], 2)
    mixing_tile = tile(mixing, halo[:, 1:], 2)
    merid_tile = tile(merid, halo[:, :1], 3)
    main_factor = factors(zonal, merid, merid_tile)
    tile_factor = factors(zonal_tile, merid_tile)
    started = diffuse(forced, mixing)
    started_tile = diffuse(forced_tile, mixing_tile)
    middle = advect(started, main_factor, started_tile) + first
    middle_tile = advect(started_tile, tile_factor) + first_tile
    mixed = diffuse(middle, mixing)
    mixed_tile = diffuse(middle_tile, mixing_tile)
    adjoint = advect(mixed, main_factor, mixed_tile)
    surface = forced + middle
    for block in range(blocks):
        span = slice(block * cells, (block + 1) * cells)
        own = adjoint[block].reshape(16, cells)
        all_ref[block] = own
        vec_ref[:16, span] = own.astype(jnp.bfloat16)
        pair = jnp.concatenate([surface[block, 0, :1], surface[block, 1, :1]], 0)
        vec_ref[16:18, span] = pair.astype(jnp.bfloat16)
    adjoint_ref[...] = all_ref[me]


def band_vectors(band, rows, cols, blocks, exchanged):
    cells = rows * cols
    return pl.pallas_call(
        functools.partial(band_kernel, rows, cols, blocks, exchanged),
        out_shape=(jax.ShapeDtypeStruct((18, blocks * cells), jnp.bfloat16), jax.ShapeDtypeStruct((16, cells), jnp.float32)),
        in_specs=[pl.BlockSpec(memory_space=pltpu.VMEM)] * len(band),
        out_specs=(pl.BlockSpec(memory_space=pltpu.VMEM), pl.BlockSpec(memory_space=pltpu.VMEM)),
        scratch_shapes=[pltpu.VMEM((blocks, 16, cells), jnp.float32)],
        compiler_params=pltpu.CompilerParams(vmem_limit_bytes=GRANT * (1 if exchanged else 4)),
        name="band",
    )(*band)


def moved(value, target):
    lats, lons = lax.axis_size("lat"), lax.axis_size("lon")
    pairs = []
    for lat in range(lats):
        for lon in range(lons):
            to_lat, to_lon = target(lat, lon)
            pairs.append((lat * lons + lon, to_lat % lats * lons + to_lon))
    return lax.ppermute(value, ("lat", "lon"), pairs)


def along_lat(nearer, farther):
    farther = moved(farther, lambda lat, lon: (lat + 1 if lat % 2 else lat - 1, lon ^ EDGE_CROSS))
    nearer = moved(nearer, lambda lat, lon: (lat ^ 1, lon ^ EDGE_CROSS))
    return nearer + farther


def gathered(main, halo):
    peers = lax.axis_size("lon")
    packed = jnp.concatenate([main, halo], 0)
    if peers > 2 * DIRECT:
        return (lax.all_gather(packed, "lon", axis=0),), False
    pieces = [packed]
    for apart in range(2, peers, 2):
        target = lambda lat, lon: (lat, lon ^ apart ^ CHIP_CROSS)
        if apart in EARLY:
            ahead = moved(main, target)
            behind = moved(halo, target)
            pieces.append(jnp.concatenate([ahead, behind], 0))
        else:
            pieces.append(moved(packed, target))
    same = jnp.stack(pieces)
    return (same, moved(same, lambda lat, lon: (lat, lon ^ 1))), True


def sum_kernel(own_ref, *refs):
    *piece_refs, state_hbm, flux_hbm, state_ref, flux_ref, sems = refs
    value = own_ref[0]
    for piece_ref in piece_refs:
        value = value + piece_ref[0]
    rows = state_ref.shape[0] * state_ref.shape[1]
    state_ref[...] = value[:rows].reshape(state_ref.shape)
    flux_ref[...] = value[rows:].reshape(flux_ref.shape)
    copies = [pltpu.make_async_copy(state_ref, state_hbm, sems.at[0]), pltpu.make_async_copy(flux_ref, flux_hbm, sems.at[1])]
    for copy in copies:
        copy.start()
    for copy in copies:
        copy.wait()


def product(vectors, panel):
    return jnp.einsum("rc,cam->arm", vectors, panel, preferred_element_type=jnp.float32)


def scattered(vectors, panel, opposite, levels):
    peers, columns = panel.shape[1:]
    shapes = ((2, levels, 1, columns), (2, 1, columns))
    if opposite is None:
        value = lax.psum_scatter(product(vectors, panel), "lat", scatter_dimension=0, tiled=True)[0]
        return value[:16].reshape(shapes[0]), value[16:].reshape(shapes[1])
    me = lax.axis_index("lat")
    total = product(vectors, opposite)
    own = product(vectors, panel)
    pieces = [lax.dynamic_slice_in_dim(own, me, 1, 0)]
    for apart in range(1, peers):
        piece = lax.dynamic_slice_in_dim(total, me ^ apart, 1, 0)
        pieces.append(moved(piece, lambda lat, lon: (lat ^ apart, lon ^ 1)))
    return pl.pallas_call(
        sum_kernel,
        out_shape=[jax.ShapeDtypeStruct(shape, jnp.float32) for shape in shapes],
        in_specs=[pl.BlockSpec(memory_space=pltpu.VMEM)] * peers,
        out_specs=[pl.BlockSpec(memory_space=pltpu.HBM)] * 2,
        scratch_shapes=[pltpu.VMEM(shape, jnp.float32) for shape in shapes] + [pltpu.SemaphoreType.DMA((2,))],
        compiler_params=pltpu.CompilerParams(vmem_limit_bytes=GRANT),
        name="total",
    )(*pieces)


def shards(forcing, zonal, meridional, mixing, panel):
    levels, rows, cols = zonal.shape
    main, nearer, farther = packed_fields(forcing, zonal, meridional, mixing)
    opposite = None
    if panel.shape[1] <= DIRECT:
        opposite = moved(with_layout_constraint(panel, Layout((0, 1, 2))), lambda lat, lon: (lat, lon ^ 1))
        opposite = with_layout_constraint(opposite, Layout((0, 1, 2)))
    band, exchanged = gathered(main, along_lat(nearer, farther))
    vectors, adjoint = band_vectors(band, rows, cols, lax.axis_size("lon"), exchanged)
    state_grad, flux_grad = scattered(vectors, panel, opposite, levels)
    adjoint_state = adjoint.reshape(2, levels, rows, cols)
    return (adjoint_state, state_grad, flux_grad)


def solution(mesh):
    return jax.shard_map(
        shards,
        mesh=mesh,
        in_specs=(
            P(None, None, None, "lat", "lon"),
            P(None, "lat", "lon"),
            P(None, "lat", "lon"),
            P(None, "lat", "lon"),
            P("lat", None, "lon"),
        ),
        out_specs=(P(None, None, "lat", "lon"), P(None, None, "lat", "lon"), P(None, "lat", "lon")),
        check_vma=False,
    )
```

```python
import functools
import jax
import jax.numpy as jnp
from jax import lax
from jax.experimental import pallas as pl
from jax.experimental.layout import Layout, with_layout_constraint
from jax.experimental.pallas import tpu as pltpu
from jax.sharding import PartitionSpec as P


DIRECT = 4
GRANT = 4 << 20
EDGE_CROSS = 1
CHIP_CROSS = 1
EARLY = (4,)


def roll(value, shift, axis=-1):
    axis %= value.ndim
    return pltpu.roll(value, shift % value.shape[axis], axis)


def pack_kernel(rows, cols, forcing_hbm, zonal_hbm, merid_hbm, mixing_hbm, main_ref, near_ref, far_ref,
                forcing_ref, zonal_ref, merid_ref, mixing_ref, sems):
    levels = zonal_hbm.shape[0] // cols
    copies = [
        pltpu.make_async_copy(source, target, sems.at[i])
        for i, (source, target) in enumerate(
            ((forcing_hbm, forcing_ref), (zonal_hbm, zonal_ref), (merid_hbm, merid_ref), (mixing_hbm, mixing_ref)))
    ]
    for copy in copies:
        copy.start()
    cells = rows * cols
    lane = lax.broadcasted_iota(jnp.int32, (2, 8, cells), 2)
    row = lane % rows

    def flat(ref, start, count=levels):
        pieces = [ref[pl.ds(start * cols + column, count, stride=cols), :] for column in range(cols)]
        return jnp.concatenate(pieces, 1)

    copies[0].wait()
    first = jnp.stack([flat(forcing_ref, 0), flat(forcing_ref, levels)])
    forced = jnp.stack([flat(forcing_ref, 2 * levels), flat(forcing_ref, 3 * levels)])
    copies[1].wait()
    copies[3].wait()
    mixing = jnp.concatenate([flat(mixing_ref, 0, levels - 1), jnp.zeros((1, cells), jnp.float32)], 0)
    pair = jnp.stack([flat(zonal_ref, 0), mixing])
    copies[2].wait()
    place = lax.axis_index("lat")
    top = jnp.where(place == lax.axis_size("lat") - 1, 1, 0)
    merid = jnp.where((row[0] == rows - 1) & (top == 1), 0.0, flat(merid_ref, 0))
    lone = jnp.stack([merid, jnp.zeros_like(merid)])
    main_ref[0:16] = forced.reshape(16, cells)
    main_ref[16:32] = first.reshape(16, cells)
    main_ref[32:48] = pair.reshape(16, cells)
    main_ref[48:56] = merid
    upper = jnp.zeros((2, 8, cells), jnp.float32)
    lower = jnp.zeros((2, 8, cells), jnp.float32)
    for i, value in enumerate((forced, first, pair, lone)):
        start = 4 * i
        lower = jnp.where((row >= start) & (row < start + 2), roll(value, start), lower)
        upper = jnp.where((row >= start + 2) & (row < start + 4), roll(value, start + 4 - rows), upper)
    even = place % 2 == 0
    near_ref[...] = jnp.where(even, upper, lower).reshape(16, cells)
    ended = (place == 0) | ((place == lax.axis_size("lat") - 1) & ~even)
    far_ref[...] = jnp.where(ended, 0.0, jnp.where(even, lower, upper)).reshape(16, cells)


def packed_fields(forcing, zonal, meridional, mixing):
    _, rows, cols = zonal.shape
    cells = rows * cols
    fields = [jnp.swapaxes(v, -1, -2).reshape(-1, rows) for v in (forcing, zonal, meridional, mixing)]
    values = [pltpu.with_memory_space_constraint(v, pltpu.HBM) for v in fields]
    edge = jax.ShapeDtypeStruct((16, cells), jnp.float32)
    return pl.pallas_call(
        functools.partial(pack_kernel, rows, cols),
        out_shape=(jax.ShapeDtypeStruct((56, cells), jnp.float32), edge, edge),
        in_specs=[pl.BlockSpec(memory_space=pltpu.HBM)] * 4,
        out_specs=[pl.BlockSpec(memory_space=pltpu.VMEM)] * 3,
        scratch_shapes=[pltpu.VMEM(v.shape, jnp.float32) for v in fields] + [pltpu.SemaphoreType.DMA((4,))],
        compiler_params=pltpu.CompilerParams(vmem_limit_bytes=GRANT),
        name="pack",
    )(*values)


def band_kernel(rows, cols, blocks, exchanged, *refs):
    *band_refs, vec_ref, adjoint_ref, all_ref = refs
    me = lax.axis_index("lon")
    cells = rows * cols
    mains, halos = [], []
    if exchanged:
        same, other = band_refs
        for chip in range(blocks // 2):
            place = jnp.bitwise_xor(chip, me // 2)
            turned = (me + CHIP_CROSS * jnp.where(place == 0, 0, 1)) % 2 == 1
            here, there = same[place], other[place]
            pair = [jnp.where(turned, there, here), jnp.where(turned, here, there)]
            mains += [piece[:56] for piece in pair]
            halos += [piece[56:] for piece in (pair[::-1] if EDGE_CROSS else pair)]
    else:
        mains = [band_refs[0][block, :56] for block in range(blocks)]
        halos = [band_refs[0][block ^ EDGE_CROSS, 56:] for block in range(blocks)]

    def field(start, count):
        return jnp.stack([block[start : start + 8 * count].reshape(count, 8, cells) for block in mains])

    forced, first, zonal, merid, mixing = field(0, 2), field(16, 2), field(32, 1), field(48, 1), field(40, 1)
    halo = jnp.stack([block.reshape(2, 8, cells) for block in halos])
    lane = lax.broadcasted_iota(jnp.int32, (1, 1, 8, cells), 3)
    row = lane % rows

    def slots(main, source, place, base):
        beyond = roll(source, base + 2 - 4 * place)
        value = jnp.where(row < base + 6, beyond, roll(main, base + 6))
        return jnp.where(row < base + 2, roll(main, base + 2 - rows), value)

    def joined(main, source, place):
        value = slots(main[:, :1], source[:, :1], place, 0)
        return jnp.where(row < 8, value, slots(main[:, 1:], source[:, 1:], place, 8))

    def doubled(main, source, place):
        value = slots(main, source, place, 0)
        return jnp.where(row < 8, value, roll(value, 8))

    def rotated(value, by):
        return jnp.concatenate([value[by:], value[:by]], 0)

    def east(value):
        turned = roll(value, -rows)
        return jnp.where(lane >= cells - rows, rotated(turned, 1), turned)

    def west(value):
        turned = roll(value, rows)
        return jnp.where(lane < rows, rotated(turned, -1), turned)

    def north(value, edge=None):
        turned = roll(value, -1)
        return turned if edge is None else jnp.where(row == rows - 1, apart(edge, value, rows - 3, rows - 11), turned)

    def south(value, edge=None):
        turned = roll(value, 1)
        return turned if edge is None else jnp.where(row == 0, apart(edge, value, -5, -13), turned)

    def apart(edge, value, one, another):
        pieces = [roll(edge, shift) for shift in (one, another)[: value.shape[1]]]
        return jnp.concatenate(pieces, 1)

    def diffuse(value, mix):
        flow = mix * (roll(value, -1, -2) - value)
        return value + flow - roll(flow, 1, -2)

    def factors(across, along, edge=None):
        out_east = jnp.maximum(across, 0.0)
        in_west = jnp.minimum(west(across), 0.0)
        out_north = jnp.maximum(along, 0.0)
        in_south = jnp.minimum(south(along, edge), 0.0)
        return (1.0 - out_east + in_west - out_north + in_south, out_east, in_west, out_north, in_south)

    def advect(value, factor, edge=None):
        centre, out_east, in_west, out_north, in_south = factor
        return (value * centre + east(value) * out_east - west(value) * in_west
                + north(value, edge) * out_north - south(value, edge) * in_south)

    forced_tile = joined(forced, halo, 0)
    first_tile = joined(first, halo, 1)
    zonal_tile = doubled(zonal, halo[:, :1], 2)
    mixing_tile = doubled(mixing, halo[:, 1:], 2)
    merid_tile = doubled(merid, halo[:, :1], 3)
    main_factor = factors(zonal, merid, merid_tile)
    tile_factor = factors(zonal_tile, merid_tile)
    started = diffuse(forced, mixing)
    started_tile = diffuse(forced_tile, mixing_tile)
    middle = advect(started, main_factor, started_tile) + first
    middle_tile = advect(started_tile, tile_factor) + first_tile
    mixed = diffuse(middle, mixing)
    mixed_tile = diffuse(middle_tile, mixing_tile)
    adjoint = advect(mixed, main_factor, mixed_tile)
    surface = forced[:, :, :1] + middle[:, :, :1]
    for block in range(blocks):
        all_ref[block] = adjoint[block].reshape(16, cells)
    adjoint_ref[...] = all_ref[me]
    source = lax.broadcasted_iota(jnp.int32, (cells, cells), 0)
    target = lax.broadcasted_iota(jnp.int32, (cells, cells), 1)
    order = jnp.where(source == (target % cols) * rows + target // cols, 1.0, 0.0).astype(jnp.bfloat16)
    fluxes = [surface[block, species] for block in range(blocks) for species in range(2)]
    stacked = jnp.concatenate([adjoint.reshape(16 * blocks, cells)] + fluxes, 0).astype(jnp.bfloat16)
    ordered = jnp.dot(stacked, order, preferred_element_type=jnp.float32).astype(jnp.bfloat16)
    for block in range(blocks):
        span = slice(block * cells, (block + 1) * cells)
        vec_ref[:16, span] = ordered[16 * block : 16 * block + 16]
        vec_ref[16:18, span] = ordered[16 * blocks + 2 * block : 16 * blocks + 2 * block + 2]


def band_vectors(band, rows, cols, blocks, exchanged):
    cells = rows * cols
    return pl.pallas_call(
        functools.partial(band_kernel, rows, cols, blocks, exchanged),
        out_shape=(jax.ShapeDtypeStruct((18, blocks * cells), jnp.bfloat16), jax.ShapeDtypeStruct((16, cells), jnp.float32)),
        in_specs=[pl.BlockSpec(memory_space=pltpu.VMEM)] * len(band),
        out_specs=(pl.BlockSpec(memory_space=pltpu.VMEM), pl.BlockSpec(memory_space=pltpu.VMEM)),
        scratch_shapes=[pltpu.VMEM((blocks, 16, cells), jnp.float32)],
        compiler_params=pltpu.CompilerParams(vmem_limit_bytes=GRANT * (1 if exchanged else 4)),
        name="band",
    )(*band)


def moved(value, target):
    lats, lons = lax.axis_size("lat"), lax.axis_size("lon")
    pairs = []
    for lat in range(lats):
        for lon in range(lons):
            to_lat, to_lon = target(lat, lon)
            pairs.append((lat * lons + lon, to_lat % lats * lons + to_lon))
    return lax.ppermute(value, ("lat", "lon"), pairs)


def along_lat(nearer, farther):
    farther = moved(farther, lambda lat, lon: (lat + 1 if lat % 2 else lat - 1, lon ^ EDGE_CROSS))
    nearer = moved(nearer, lambda lat, lon: (lat ^ 1, lon ^ EDGE_CROSS))
    return nearer + farther


def gathered(main, halo):
    peers = lax.axis_size("lon")
    packed = jnp.concatenate([main, halo], 0)
    if peers > 2 * DIRECT:
        return (lax.all_gather(packed, "lon", axis=0),), False
    pieces = [packed]
    for apart in range(2, peers, 2):
        target = lambda lat, lon: (lat, lon ^ apart ^ CHIP_CROSS)
        if apart in EARLY:
            ahead = moved(main, target)
            behind = moved(halo, target)
            pieces.append(jnp.concatenate([ahead, behind], 0))
        else:
            pieces.append(moved(packed, target))
    same = jnp.stack(pieces)
    return (same, moved(same, lambda lat, lon: (lat, lon ^ 1))), True


def sum_kernel(own_ref, *refs):
    *piece_refs, state_hbm, flux_hbm, state_ref, flux_ref, sems = refs
    value = own_ref[0]
    for piece_ref in piece_refs:
        value = value + piece_ref[0]
    rows = state_ref.shape[0] * state_ref.shape[1]
    state_ref[...] = value[:rows].reshape(state_ref.shape)
    flux_ref[...] = value[rows:].reshape(flux_ref.shape)
    copies = [pltpu.make_async_copy(state_ref, state_hbm, sems.at[0]), pltpu.make_async_copy(flux_ref, flux_hbm, sems.at[1])]
    for copy in copies:
        copy.start()
    for copy in copies:
        copy.wait()


def product(vectors, panel):
    return jnp.einsum("rc,cam->arm", vectors, panel, preferred_element_type=jnp.float32)


def scattered(vectors, panel, opposite, levels):
    peers, columns = panel.shape[1:]
    shapes = ((2, levels, 1, columns), (2, 1, columns))
    if opposite is None:
        value = lax.psum_scatter(product(vectors, panel), "lat", scatter_dimension=0, tiled=True)[0]
        return value[:16].reshape(shapes[0]), value[16:].reshape(shapes[1])
    me = lax.axis_index("lat")
    total = product(vectors, opposite)
    own = product(vectors, panel)
    pieces = [lax.dynamic_slice_in_dim(own, me, 1, 0)]
    for apart in range(1, peers):
        piece = lax.dynamic_slice_in_dim(total, me ^ apart, 1, 0)
        pieces.append(moved(piece, lambda lat, lon: (lat ^ apart, lon ^ 1)))
    return pl.pallas_call(
        sum_kernel,
        out_shape=[jax.ShapeDtypeStruct(shape, jnp.float32) for shape in shapes],
        in_specs=[pl.BlockSpec(memory_space=pltpu.VMEM)] * peers,
        out_specs=[pl.BlockSpec(memory_space=pltpu.HBM)] * 2,
        scratch_shapes=[pltpu.VMEM(shape, jnp.float32) for shape in shapes] + [pltpu.SemaphoreType.DMA((2,))],
        compiler_params=pltpu.CompilerParams(vmem_limit_bytes=GRANT),
        name="total",
    )(*pieces)


def shards(forcing, zonal, meridional, mixing, panel):
    levels, rows, cols = zonal.shape
    main, nearer, farther = packed_fields(forcing, zonal, meridional, mixing)
    opposite = None
    if panel.shape[1] <= DIRECT:
        opposite = moved(with_layout_constraint(panel, Layout((0, 1, 2))), lambda lat, lon: (lat, lon ^ 1))
        opposite = with_layout_constraint(opposite, Layout((0, 1, 2)))
    band, exchanged = gathered(main, along_lat(nearer, farther))
    vectors, adjoint = band_vectors(band, rows, cols, lax.axis_size("lon"), exchanged)
    state_grad, flux_grad = scattered(vectors, panel, opposite, levels)
    adjoint_state = jnp.swapaxes(adjoint.reshape(2, levels, cols, rows), 2, 3)
    return (adjoint_state, state_grad, flux_grad)


def solution(mesh):
    return jax.shard_map(
        shards,
        mesh=mesh,
        in_specs=(
            P(None, None, None, "lat", "lon"),
            P(None, "lat", "lon"),
            P(None, "lat", "lon"),
            P(None, "lat", "lon"),
            P("lat", None, "lon"),
        ),
        out_specs=(P(None, None, "lat", "lon"), P(None, None, "lat", "lon"), P(None, "lat", "lon")),
        check_vma=False,
    )
```

```python
import functools
import jax
import jax.numpy as jnp
from jax import lax
from jax.experimental import pallas as pl
from jax.experimental.layout import Layout, with_layout_constraint
from jax.experimental.pallas import tpu as pltpu
from jax.sharding import PartitionSpec as P


DIRECT = 4
GRANT = 4 << 20
EDGE_CROSS = 1
CHIP_CROSS = 1
EARLY = (4,)


def roll(value, shift, axis=-1):
    axis %= value.ndim
    return pltpu.roll(value, shift % value.shape[axis], axis)


def pack_kernel(rows, cols, forcing_hbm, zonal_hbm, merid_hbm, mixing_hbm, main_ref, near_ref, far_ref,
                forcing_ref, zonal_ref, merid_ref, mixing_ref, sems):
    levels = zonal_hbm.shape[0] // cols
    copies = [
        pltpu.make_async_copy(source, target.at[pl.ds(0, source.shape[0])], sems.at[i])
        for i, (source, target) in enumerate(
            ((forcing_hbm, forcing_ref), (zonal_hbm, zonal_ref), (merid_hbm, merid_ref), (mixing_hbm, mixing_ref)))
    ]
    for copy in copies:
        copy.start()
    cells = rows * cols
    lane = lax.broadcasted_iota(jnp.int32, (2, 8, cells), 2)
    row = lane % rows

    def flat(ref, start, count=levels):
        pieces = [ref[pl.ds(start * cols + column, count, stride=cols), :] for column in range(cols)]
        return jnp.concatenate(pieces, 1)

    copies[0].wait()
    first = jnp.stack([flat(forcing_ref, 0), flat(forcing_ref, levels)])
    forced = jnp.stack([flat(forcing_ref, 2 * levels), flat(forcing_ref, 3 * levels)])
    copies[1].wait()
    copies[3].wait()
    mixing = jnp.concatenate([flat(mixing_ref, 0, levels - 1), jnp.zeros((1, cells), jnp.float32)], 0)
    pair = jnp.stack([flat(zonal_ref, 0), mixing])
    copies[2].wait()
    place = lax.axis_index("lat")
    top = jnp.where(place == lax.axis_size("lat") - 1, 1, 0)
    merid = jnp.where((row[0] == rows - 1) & (top == 1), 0.0, flat(merid_ref, 0))
    lone = jnp.stack([merid, jnp.zeros_like(merid)])
    main_ref[0:16] = forced.reshape(16, cells)
    main_ref[16:32] = first.reshape(16, cells)
    main_ref[32:48] = pair.reshape(16, cells)
    main_ref[48:56] = merid
    upper = jnp.zeros((2, 8, cells), jnp.float32)
    lower = jnp.zeros((2, 8, cells), jnp.float32)
    for i, value in enumerate((forced, first, pair, lone)):
        start = 4 * i
        lower = jnp.where((row >= start) & (row < start + 2), roll(value, start), lower)
        upper = jnp.where((row >= start + 2) & (row < start + 4), roll(value, start + 4 - rows), upper)
    even = place % 2 == 0
    near_ref[...] = jnp.where(even, upper, lower).reshape(16, cells)
    ended = (place == 0) | ((place == lax.axis_size("lat") - 1) & ~even)
    far_ref[...] = jnp.where(ended, 0.0, jnp.where(even, lower, upper)).reshape(16, cells)


def packed_fields(forcing, zonal, meridional, mixing):
    _, rows, cols = zonal.shape
    cells = rows * cols
    fields = [jnp.swapaxes(v, -1, -2).reshape(-1, rows) for v in (forcing, zonal, meridional, mixing)]
    values = [pltpu.with_memory_space_constraint(v, pltpu.HBM) for v in fields]
    edge = jax.ShapeDtypeStruct((16, cells), jnp.float32)
    return pl.pallas_call(
        functools.partial(pack_kernel, rows, cols),
        out_shape=(jax.ShapeDtypeStruct((56, cells), jnp.float32), edge, edge),
        in_specs=[pl.BlockSpec(memory_space=pltpu.HBM)] * 4,
        out_specs=[pl.BlockSpec(memory_space=pltpu.VMEM)] * 3,
        scratch_shapes=[pltpu.VMEM((v.shape[0] + 2 * cols, rows), jnp.float32) for v in fields] + [pltpu.SemaphoreType.DMA((4,))],
        compiler_params=pltpu.CompilerParams(vmem_limit_bytes=GRANT),
        name="pack",
    )(*values)


def band_kernel(rows, cols, blocks, exchanged, *refs):
    *band_refs, vec_ref, adjoint_ref, all_ref = refs
    me = lax.axis_index("lon")
    cells = rows * cols
    mains, halos = [], []
    if exchanged:
        same, other = band_refs
        for chip in range(blocks // 2):
            place = jnp.bitwise_xor(chip, me // 2)
            turned = (me + CHIP_CROSS * jnp.where(place == 0, 0, 1)) % 2 == 1
            here, there = same[place], other[place]
            pair = [jnp.where(turned, there, here), jnp.where(turned, here, there)]
            mains += [piece[:56] for piece in pair]
            halos += [piece[56:] for piece in (pair[::-1] if EDGE_CROSS else pair)]
    else:
        mains = [band_refs[0][block, :56] for block in range(blocks)]
        halos = [band_refs[0][block ^ EDGE_CROSS, 56:] for block in range(blocks)]

    def field(start, count):
        return jnp.stack([block[start : start + 8 * count].reshape(count, 8, cells) for block in mains])

    forced, first, zonal, merid, mixing = field(0, 2), field(16, 2), field(32, 1), field(48, 1), field(40, 1)
    halo = jnp.stack([block.reshape(2, 8, cells) for block in halos])
    lane = lax.broadcasted_iota(jnp.int32, (1, 1, 8, cells), 3)
    row = lane % rows

    def slots(main, source, place, base):
        beyond = roll(source, base + 2 - 4 * place)
        value = jnp.where(row < base + 6, beyond, roll(main, base + 6))
        return jnp.where(row < base + 2, roll(main, base + 2 - rows), value)

    def joined(main, source, place):
        value = slots(main[:, :1], source[:, :1], place, 0)
        return jnp.where(row < 8, value, slots(main[:, 1:], source[:, 1:], place, 8))

    def doubled(main, source, place):
        value = slots(main, source, place, 0)
        return jnp.where(row < 8, value, roll(value, 8))

    def rotated(value, by):
        return jnp.concatenate([value[by:], value[:by]], 0)

    def east(value):
        turned = roll(value, -rows)
        return jnp.where(lane >= cells - rows, rotated(turned, 1), turned)

    def west(value):
        turned = roll(value, rows)
        return jnp.where(lane < rows, rotated(turned, -1), turned)

    def north(value, edge=None):
        turned = roll(value, -1)
        return turned if edge is None else jnp.where(row == rows - 1, apart(edge, value, rows - 3, rows - 11), turned)

    def south(value, edge=None):
        turned = roll(value, 1)
        return turned if edge is None else jnp.where(row == 0, apart(edge, value, -5, -13), turned)

    def apart(edge, value, one, another):
        pieces = [roll(edge, shift) for shift in (one, another)[: value.shape[1]]]
        return jnp.concatenate(pieces, 1)

    def diffuse(value, mix):
        flow = mix * (roll(value, -1, -2) - value)
        return value + flow - roll(mix, 1, -2) * (value - roll(value, 1, -2))

    def factors(across, along, edge=None):
        out_east = jnp.maximum(across, 0.0)
        in_west = jnp.minimum(west(across), 0.0)
        out_north = jnp.maximum(along, 0.0)
        in_south = jnp.minimum(south(along, edge), 0.0)
        return (1.0 - out_east + in_west - out_north + in_south, out_east, in_west, out_north, in_south)

    def advect(value, factor, edge=None):
        centre, out_east, in_west, out_north, in_south = factor
        return (value * centre + east(value) * out_east - west(value) * in_west
                + north(value, edge) * out_north - south(value, edge) * in_south)

    forced_tile = joined(forced, halo, 0)
    first_tile = joined(first, halo, 1)
    zonal_tile = doubled(zonal, halo[:, :1], 2)
    mixing_tile = doubled(mixing, halo[:, 1:], 2)
    merid_tile = doubled(merid, halo[:, :1], 3)
    main_factor = factors(zonal, merid, merid_tile)
    tile_factor = factors(zonal_tile, merid_tile)
    started = diffuse(forced, mixing)
    started_tile = diffuse(forced_tile, mixing_tile)
    middle = advect(started, main_factor, started_tile) + first
    middle_tile = advect(started_tile, tile_factor) + first_tile
    mixed = diffuse(middle, mixing)
    mixed_tile = diffuse(middle_tile, mixing_tile)
    adjoint = advect(mixed, main_factor, mixed_tile)
    surface = forced[:, :, :1] + middle[:, :, :1]
    for block in range(blocks):
        all_ref[block] = adjoint[block].reshape(16, cells)
    adjoint_ref[...] = all_ref[me]
    source = lax.broadcasted_iota(jnp.int32, (cells, cells), 0)
    target = lax.broadcasted_iota(jnp.int32, (cells, cells), 1)
    order = jnp.where(source == (target % cols) * rows + target // cols, 1.0, 0.0).astype(jnp.bfloat16)
    fluxes = [surface[block, species] for block in range(blocks) for species in range(2)]
    stacked = jnp.concatenate([adjoint.reshape(16 * blocks, cells)] + fluxes, 0).astype(jnp.bfloat16)
    ordered = jnp.dot(stacked, order, preferred_element_type=jnp.float32).astype(jnp.bfloat16)
    for block in range(blocks):
        span = slice(block * cells, (block + 1) * cells)
        vec_ref[:16, span] = ordered[16 * block : 16 * block + 16]
        vec_ref[16:18, span] = ordered[16 * blocks + 2 * block : 16 * blocks + 2 * block + 2]


def band_vectors(band, rows, cols, blocks, exchanged):
    cells = rows * cols
    return pl.pallas_call(
        functools.partial(band_kernel, rows, cols, blocks, exchanged),
        out_shape=(jax.ShapeDtypeStruct((18, blocks * cells), jnp.bfloat16), jax.ShapeDtypeStruct((16, cells), jnp.float32)),
        in_specs=[pl.BlockSpec(memory_space=pltpu.VMEM)] * len(band),
        out_specs=(pl.BlockSpec(memory_space=pltpu.VMEM), pl.BlockSpec(memory_space=pltpu.VMEM)),
        scratch_shapes=[pltpu.VMEM((blocks, 16, cells), jnp.float32)],
        compiler_params=pltpu.CompilerParams(vmem_limit_bytes=GRANT * (1 if exchanged else 4)),
        name="band",
    )(*band)


def moved(value, target):
    lats, lons = lax.axis_size("lat"), lax.axis_size("lon")
    pairs = []
    for lat in range(lats):
        for lon in range(lons):
            to_lat, to_lon = target(lat, lon)
            pairs.append((lat * lons + lon, to_lat % lats * lons + to_lon))
    return lax.ppermute(value, ("lat", "lon"), pairs)


def along_lat(nearer, farther):
    ends = (0, lax.axis_size("lat") - 1)
    farther = moved(farther, lambda lat, lon: (
        (lat, lon ^ 1) if lat in ends else (lat + 1 if lat % 2 else lat - 1, lon ^ EDGE_CROSS)))
    nearer = moved(nearer, lambda lat, lon: (lat ^ 1, lon ^ EDGE_CROSS))
    return nearer + farther


def gathered(main, halo):
    peers = lax.axis_size("lon")
    packed = jnp.concatenate([main, halo], 0)
    if peers > 2 * DIRECT:
        return (lax.all_gather(packed, "lon", axis=0),), False
    pieces = {}
    for apart in range(2, peers, 2):
        target = lambda lat, lon: (lat, lon ^ apart ^ CHIP_CROSS)
        if apart in EARLY:
            ahead = moved(main, target)
            behind = moved(halo, target)
            pieces[apart] = jnp.concatenate([ahead, behind], 0)
        else:
            pieces[apart] = moved(packed, target)
    also = moved(packed, lambda lat, lon: (lat, lon ^ 2 ^ 1 ^ CHIP_CROSS))
    far = [pieces[apart] for apart in range(4, peers, 2)]
    swapped = moved(jnp.stack([packed] + far), lambda lat, lon: (lat, lon ^ 1))
    same = jnp.stack([packed, pieces[2]] + far)
    return (same, jnp.concatenate([swapped[:1], also[None], swapped[1:]], 0)), True


def sum_kernel(own_ref, *refs):
    *piece_refs, state_hbm, flux_hbm, state_ref, flux_ref, sems = refs
    value = own_ref[0]
    for piece_ref in piece_refs:
        value = value + piece_ref[0]
    rows = state_ref.shape[0] * state_ref.shape[1]
    state_ref[...] = value[:rows].reshape(state_ref.shape)
    flux_ref[...] = value[rows:].reshape(flux_ref.shape)
    copies = [pltpu.make_async_copy(state_ref, state_hbm, sems.at[0]), pltpu.make_async_copy(flux_ref, flux_hbm, sems.at[1])]
    for copy in copies:
        copy.start()
    for copy in copies:
        copy.wait()


def product(vectors, panel):
    return jnp.einsum("rc,cam->arm", vectors, panel, preferred_element_type=jnp.float32)


def scattered(vectors, panel, opposite, levels):
    peers, columns = panel.shape[1:]
    shapes = ((2, levels, 1, columns), (2, 1, columns))
    if opposite is None:
        value = lax.psum_scatter(product(vectors, panel), "lat", scatter_dimension=0, tiled=True)[0]
        return value[:16].reshape(shapes[0]), value[16:].reshape(shapes[1])
    me = lax.axis_index("lat")
    total = product(vectors, opposite)
    own = product(vectors, panel)
    pieces = [lax.dynamic_slice_in_dim(own, me, 1, 0)]
    for apart in range(1, peers):
        piece = lax.dynamic_slice_in_dim(total, me ^ apart, 1, 0)
        pieces.append(moved(piece, lambda lat, lon: (lat ^ apart, lon ^ 1)))
    return pl.pallas_call(
        sum_kernel,
        out_shape=[jax.ShapeDtypeStruct(shape, jnp.float32) for shape in shapes],
        in_specs=[pl.BlockSpec(memory_space=pltpu.VMEM)] * peers,
        out_specs=[pl.BlockSpec(memory_space=pltpu.HBM)] * 2,
        scratch_shapes=[pltpu.VMEM(shape, jnp.float32) for shape in shapes] + [pltpu.SemaphoreType.DMA((2,))],
        compiler_params=pltpu.CompilerParams(vmem_limit_bytes=GRANT),
        name="total",
    )(*pieces)


def shards(forcing, zonal, meridional, mixing, panel):
    levels, rows, cols = zonal.shape
    main, nearer, farther = packed_fields(forcing, zonal, meridional, mixing)
    opposite = None
    if panel.shape[1] <= DIRECT:
        opposite = moved(with_layout_constraint(panel, Layout((0, 1, 2))), lambda lat, lon: (lat, lon ^ 1))
        opposite = with_layout_constraint(opposite, Layout((0, 1, 2)))
    band, exchanged = gathered(main, along_lat(nearer, farther))
    vectors, adjoint = band_vectors(band, rows, cols, lax.axis_size("lon"), exchanged)
    state_grad, flux_grad = scattered(vectors, panel, opposite, levels)
    adjoint_state = jnp.swapaxes(adjoint.reshape(2, levels, cols, rows), 2, 3)
    return (adjoint_state, state_grad, flux_grad)


def solution(mesh):
    return jax.shard_map(
        shards,
        mesh=mesh,
        in_specs=(
            P(None, None, None, "lat", "lon"),
            P(None, "lat", "lon"),
            P(None, "lat", "lon"),
            P(None, "lat", "lon"),
            P("lat", None, "lon"),
        ),
        out_specs=(P(None, None, "lat", "lon"), P(None, None, "lat", "lon"), P(None, "lat", "lon")),
        check_vma=False,
    )
```
